32 devices in a mesh: dp: 16 (over z, y, core), seq: 2 (over x).
Axes of the slice: x: 2, y: 2, z: 4, core: 2. Of those that a mesh axis runs over, the one named last changes fastest.
Arguments:
- tokens: bfloat16 [16, 512, 1024], P('dp', 'seq'), may hold values from -6 to 6
- first_values: bfloat16 [16, 512, 1024], P('dp', 'seq'), may hold values from -6 to 6
- doc_ids: int32 [16, 512], P('dp'), may hold values from 0 to 7, never falling along the last dimension, each value on 1 to 256 neighbouring positions
- cotangent: bfloat16 [16, 512, 1024], P('dp', 'seq'), may hold values from -6 to 6
- norm1_gain: bfloat16 [1024], P(('dp', 'seq')), may hold values from 0.5 to 1.5
- w_query: bfloat16 [1024, 1024], P(('dp', 'seq')), may hold values from -0.25 to 0.25
- w_key: bfloat16 [1024, 1024], P(('dp', 'seq')), may hold values from -0.25 to 0.25
- w_value: bfloat16 [1024, 1024], P(('dp', 'seq')), may hold values from -0.1875 to 0.1875
- w_out: bfloat16 [1024, 1024], P(('dp', 'seq')), may hold values from -0.75 to 0.75
- norm2_gain: bfloat16 [1024], P(('dp', 'seq')), may hold values from 0.5 to 1.5
- w_gate: bfloat16 [1024, 2816], P(('dp', 'seq')), may hold values from -0.1875 to 0.1875
- w_up: bfloat16 [1024, 2816], P(('dp', 'seq')), may hold values from -0.1875 to 0.1875
- w_down: bfloat16 [2816, 1024], P(('dp', 'seq')), may hold values from -0.21875 to 0.21875
Outputs:
- layer_out: bfloat16 [16, 512, 1024], P('dp', 'seq')
- grad_tokens: bfloat16 [16, 512, 1024], P('dp', 'seq')
- grad_first_values: bfloat16 [16, 512, 1024], P('dp', 'seq')
- grad_norm1: float32 [1024], P(('dp', 'seq'))
- grad_query: float32 [1024, 1024], P(('dp', 'seq'))
- grad_key: float32 [1024, 1024], P(('dp', 'seq'))
- grad_value: float32 [1024, 1024], P(('dp', 'seq'))
- grad_out: float32 [1024, 1024], P(('dp', 'seq'))
- grad_norm2: float32 [1024], P(('dp', 'seq'))
- grad_gate: float32 [1024, 2816], P(('dp', 'seq'))
- grad_up: float32 [1024, 2816], P(('dp', 'seq'))
- grad_down: float32 [2816, 1024], P(('dp', 'seq'))
The draws below stay inside these ranges and needn't reach their ends.
Inputs may be any that keep to these rules, and one draw needn't show every extreme that they name: `doc_ids`: along a stream the document numbers never fall; each document covers 1 to 256 positions, and in each stream one covers exactly 256.
All inputs are finite; a program needn't handle non-finite values.
Results may differ from the reference program's by a relative error of at most 0.025.
Values may be sent and summed in bfloat16 or wider, within the bound.
A program may use at most 192 MiB of HBM per device.

```python
import math
import jax
import jax.numpy as jnp
import numpy as np
from jax import lax

D = 1024
H = 16
FF = 2816
HD = 64
TOK_DEV = 256
BLOCK = 512
STREAM = 512
STREAMS = 16
N_SEQ = 2


def shard_levels(own_key, dims, pieces, least, top_value):
    level, own = 1.0, jax.random.fold_in(own_key, 6)
    for dim, shards_of in pieces:
        draws = jnp.exp(jax.random.uniform(jax.random.fold_in(own, dim), (shards_of,), jnp.float32, least / len(pieces), top_value / len(pieces)))
        level = level * jnp.repeat(draws, dims[dim] // shards_of).reshape([-1 if axis == dim else 1 for axis in range(len(dims))])
    return level


def split_up(number_of, total, bound, lean):
    loads = [(1 << 20) // math.isqrt(standing ** lean) + 1 for standing in range(2, number_of + 1)]
    surplus, given = total - bound - (number_of - 1), [1] * (number_of - 1)
    while surplus > 0:
        free = [i for i in range(number_of - 1) if given[i] < bound]
        whole, left = sum([loads[i] for i in free]), surplus
        for i in free:
            extra = min(bound - given[i], max(1, left * loads[i] // whole), surplus)
            given[i] = given[i] + extra
            surplus = surplus - extra
    return np.array([bound] + given)


def ragged(key, number_of, total, reach, skew):
    if number_of == 2:
        one = jax.random.randint(key, (), max(1, total - reach), min(reach, total - 1) + 1)
        return jnp.stack([one, total - one])
    tallies = jnp.asarray(split_up(number_of, total, reach, skew), jnp.int32)
    couples = (number_of - 1) // 2
    source_of, sink = tallies[1:1 + 2 * couples:2], tallies[2:2 + 2 * couples:2]
    room = jnp.minimum(source_of - 1, reach - sink)
    passed = jax.random.randint(jax.random.fold_in(key, 1), (couples,), 0, 1 << 20) % (room + 1)
    tallies = tallies.at[1:1 + 2 * couples:2].set(source_of - passed).at[2:2 + 2 * couples:2].set(sink + passed)
    return tallies[jax.random.permutation(jax.random.fold_in(key, 2), number_of)]


def bell_draw(key, extent, deviation, bound, cuts=(), dtype=jnp.bfloat16):
    array = jax.random.normal(key, extent, jnp.float32) * deviation
    if len(cuts) > 0:
        array = shard_levels(key, extent, cuts, -0.22, 0.18) * array
    return jnp.clip(array, min=-bound, max=bound).astype(dtype)


def setup_inputs(seed: int = 0) -> dict:
    keys = jax.random.split(jax.random.key(seed), 14)
    tokens = bell_draw(keys[0], (STREAMS, STREAM, D), 1.0, 6.0, ((0, 16), (1, 2)))
    first_values = bell_draw(keys[1], (STREAMS, STREAM, D), 1.0, 6.0, ((0, 16), (1, 2)))
    doc_ids = jax.vmap(lambda own: jnp.searchsorted(jnp.cumsum(ragged(own, 4 * N_SEQ, STREAM, TOK_DEV * N_SEQ // 2, 2)), jnp.arange(STREAM), side="right"))(jax.random.split(keys[2], STREAMS)).reshape((STREAMS, STREAM)).astype(jnp.int32)
    cotangent = bell_draw(keys[3], (STREAMS, STREAM, D), 1.0, 6.0, ((0, 16), (1, 2)))
    norm1_gain = jnp.clip(1.0 + 0.1 * jax.random.normal(keys[4], (D,), jnp.float32), 0.5, 1.5).astype(jnp.bfloat16)
    w_query = bell_draw(keys[5], (D, D), (D // 2) ** -0.5, 0.25, ((0, 32),))
    w_key = bell_draw(keys[6], (D, D), (D // 2) ** -0.5, 0.25, ((0, 32),))
    w_value = bell_draw(keys[7], (D, D), D ** -0.5, 0.1875, ((0, 32),))
    w_out = bell_draw(keys[8], (D, D), (D // 16) ** -0.5, 0.75, ((0, 32),))
    norm2_gain = jnp.clip(1.0 + 0.1 * jax.random.normal(keys[9], (D,), jnp.float32), 0.5, 1.5).astype(jnp.bfloat16)
    w_gate = bell_draw(keys[10], (D, FF), D ** -0.5, 0.1875, ((0, 32),))
    w_up = bell_draw(keys[11], (D, FF), D ** -0.5, 0.1875, ((0, 32),))
    w_down = bell_draw(keys[12], (FF, D), (FF // 4) ** -0.5, 0.21875, ((0, 32),))
    return {"tokens": tokens, "first_values": first_values, "doc_ids": doc_ids, "cotangent": cotangent, "norm1_gain": norm1_gain, "w_query": w_query, "w_key": w_key, "w_value": w_value, "w_out": w_out, "norm2_gain": norm2_gain, "w_gate": w_gate, "w_up": w_up, "w_down": w_down}


@jax.custom_vjp
def low(v):
    return lax.optimization_barrier(v.astype(jnp.bfloat16)).astype(jnp.float32)

@jax.custom_vjp
def low_back(v):
    return v

def low_keep(v):
    return (low(v), None)

def low_pass(kept, grad):
    return (grad,)

def back_keep(v):
    return (v, None)

def back_low(kept, grad):
    return (low(grad),)
low.defvjp(low_keep, low_pass)
low_back.defvjp(back_keep, back_low)

def rms_scale(h, gain):
    return h * lax.rsqrt(lax.optimization_barrier(jnp.mean(h * h, axis=-1, keepdims=True)) + 1e-05) * gain

def rotate(t, cos_tab, sin_tab):
    half = t.shape[-1] // 2
    first = t[..., :half]
    second = t[..., half:]
    return jnp.concatenate([first * cos_tab - second * sin_tab, first * sin_tab + second * cos_tab], axis=-1)

def layer(params, xs, first, segment):
    gain1, wq, wk, wv, wo, gain2, wg, wu, wd = params
    highest = lax.Precision.HIGHEST
    length = xs.shape[0]
    normed = low(rms_scale(xs, gain1))
    positions = jnp.arange(length).astype(jnp.float32)
    freqs = 10000.0 ** (-jnp.arange(HD // 2).astype(jnp.float32) * 2.0 / HD)
    angle = positions[:, None] * freqs[None, :]
    cos_tab = jnp.cos(angle)[:, None, :]
    sin_tab = jnp.sin(angle)[:, None, :]

    def split_heads(t):
        return t.reshape(length, H, HD)
    query = low(low_back(rotate(low_back(split_heads(jnp.dot(normed, wq, precision=highest))), cos_tab, sin_tab)))
    key = low(low_back(rotate(low_back(split_heads(jnp.dot(normed, wk, precision=highest))), cos_tab, sin_tab)))
    value = low(low_back(0.5 * (split_heads(jnp.dot(normed, wv, precision=highest)) + split_heads(first))))
    scale = HD ** (-0.5)
    index = jnp.arange(length).astype(jnp.int32)

    def attend(start):
        q_rows = lax.dynamic_slice_in_dim(query, start, BLOCK, 0)
        seg_rows = lax.dynamic_slice_in_dim(segment, start, BLOCK, 0)
        rows = start + jnp.arange(BLOCK).astype(jnp.int32)
        mask = (seg_rows[:, None] == segment[None, :]) & (index[None, :] <= rows[:, None])
        scores = low_back(jnp.einsum('qhd,khd->hqk', q_rows, key, precision=highest) * scale)
        scores = jnp.where(mask[None], scores, -1e+30)
        probs = low(jax.nn.softmax(scores, axis=-1))
        return jnp.einsum('hqk,khd->qhd', probs, value, precision=highest)
    starts = (jnp.arange(length // BLOCK) * BLOCK).astype(jnp.int32)
    mixed = lax.map(jax.checkpoint(attend), starts).reshape(length, D)
    mixed = low(low_back(mixed))
    attended = low_back(jnp.dot(mixed, wo, precision=highest))
    h1 = xs + attended
    normed2 = low(rms_scale(h1, gain2))
    gate = low_back(jnp.dot(normed2, wg, precision=highest))
    up = low_back(jnp.dot(normed2, wu, precision=highest))
    hidden = low(jax.nn.silu(gate) * up)
    return h1 + jnp.dot(hidden, wd, precision=highest)

def reference(tokens, first_values, doc_ids, cotangent, norm1_gain, w_query, w_key, w_value, w_out, norm2_gain, w_gate, w_up, w_down):
    params = tuple((p.astype(jnp.float32) for p in (norm1_gain, w_query, w_key, w_value, w_out, norm2_gain, w_gate, w_up, w_down)))

    def one_stream(totals, item):
        xs, first, segment, grad_out = item

        def forward(weights, inputs, values):
            return layer(weights, inputs, values, segment)
        result, pull = jax.vjp(forward, params, xs.astype(jnp.float32), first.astype(jnp.float32))
        grads, grad_x, grad_first = pull(grad_out.astype(jnp.float32))
        totals = jax.tree.map(lambda left, right: left + right, totals, grads)
        return (totals, (result.astype(jnp.bfloat16), grad_x.astype(jnp.bfloat16), grad_first.astype(jnp.bfloat16)))
    zeros = tuple((jnp.zeros_like(p) for p in params))
    totals, outputs = lax.scan(one_stream, zeros, (tokens, first_values, doc_ids, cotangent))
    return (outputs[0], outputs[1], outputs[2], totals[0], totals[1], totals[2], totals[3], totals[4], totals[5], totals[6], totals[7], totals[8])
```

```python
import functools

import jax
import jax.numpy as jnp
from jax import lax
from jax.experimental import pallas as pl
from jax.experimental.pallas import tpu as pltpu
from jax.sharding import PartitionSpec as P

H = 16
BLOCK = 512


epsilon = 1e-05


def norm_forward(h, gain):
    inverse = lax.rsqrt(jnp.mean(h * h, axis=-1, keepdims=True) + epsilon)
    return (h * inverse * gain, inverse)


def norm_backward(h, inverse, gain, grad_normed):
    scaled = grad_normed * gain
    grad_gain = jnp.sum(grad_normed * h * inverse, axis=0)
    grad_h = inverse * scaled - h * inverse * inverse * inverse * jnp.mean(
        h * scaled, axis=-1, keepdims=True
    )
    return (grad_h, grad_gain)


def rope_tables(start, count, width):
    positions = (start + jnp.arange(count, dtype=jnp.int32)).astype(jnp.float32)
    freqs = 10000.0 ** (-jnp.arange(width // 2, dtype=jnp.float32) * 2.0 / width)
    angle = positions[:, None] * freqs[None, :]
    return (jnp.cos(angle)[:, None, :], jnp.sin(angle)[:, None, :])


def rotate(t, cos_tab, sin_tab, sign):
    half = t.shape[-1] // 2
    first = t[..., :half]
    second = t[..., half:]
    return jnp.concatenate(
        [first * cos_tab - sign * second * sin_tab, sign * first * sin_tab + second * cos_tab],
        axis=-1,
    )


def seq_major(t, outer, inner):
    shape = t.shape
    lead = (outer, inner, shape[0] // (outer * inner)) + tuple(shape[1:])
    return jnp.swapaxes(t.reshape(lead), 0, 1).reshape(shape)


def matmul_left(a, b):
    return lax.dot_general(a, b, (((0,), (0,)), ((), ())), preferred_element_type=jnp.float32)


def matmul_right(a, b):
    return lax.dot_general(a, b, (((1,), (1,)), ((), ())), preferred_element_type=jnp.float32)


def per_device(
    tokens,
    first_values,
    doc_ids,
    cotangent,
    norm1_gain,
    w_query,
    w_key,
    w_value,
    w_out,
    norm2_gain,
    w_gate,
    w_up,
    w_down,
):
    groups = lax.axis_size("seq")
    outer = lax.axis_size("dp")
    rows = tokens.shape[1]
    width = tokens.shape[2]
    head_size = width // H
    local_heads = H // groups
    stream_len = rows * groups
    scale = head_size ** (-0.5)
    block_count = stream_len // BLOCK
    x_in = tokens[0].astype(jnp.float32)
    segment = doc_ids[0]
    attn_set = (
        lax.all_gather(norm1_gain, ("dp", "seq"), axis=0, tiled=True),
        lax.all_gather(w_query, ("dp", "seq"), axis=0, tiled=True),
        lax.all_gather(w_key, ("dp", "seq"), axis=0, tiled=True),
        lax.all_gather(w_value, ("dp", "seq"), axis=0, tiled=True),
        lax.all_gather(w_out, ("dp", "seq"), axis=0, tiled=True),
    )
    gain1, wq, wk, wv, wo = attn_set
    gain1_f = gain1.astype(jnp.float32)
    normed1, inverse1 = norm_forward(x_in, gain1_f)
    normed1_b = normed1.astype(jnp.bfloat16)
    cos_tab, sin_tab = rope_tables(lax.axis_index("seq") * rows, rows, head_size)

    def project(weight):
        return jnp.dot(normed1_b, weight, preferred_element_type=jnp.float32).reshape(
            rows, H, head_size
        )

    query_b = rotate(project(wq), cos_tab, sin_tab, 1.0).astype(jnp.bfloat16)
    key_b = rotate(project(wk), cos_tab, sin_tab, 1.0).astype(jnp.bfloat16)
    first_f = first_values[0].astype(jnp.float32).reshape(rows, H, head_size)
    value_b = (0.5 * (project(wv) + first_f)).astype(jnp.bfloat16)

    def slice_layout(t):
        return t.reshape(rows, groups, local_heads * head_size)

    def head_layout(t):
        return t.reshape(stream_len, local_heads, head_size)

    query_h, key_h, value_h = (
        lax.all_to_all(slice_layout(query_b), "seq", split_axis=1, concat_axis=0, tiled=True),
        lax.all_to_all(slice_layout(key_b), "seq", split_axis=1, concat_axis=0, tiled=True),
        lax.all_to_all(slice_layout(value_b), "seq", split_axis=1, concat_axis=0, tiled=True),
    )
    query_h = head_layout(query_h)
    key_h = head_layout(key_h)
    value_h = head_layout(value_h)
    positions = jnp.arange(stream_len, dtype=jnp.int32)

    def block_scores(q_rows, start):
        seg_rows = lax.dynamic_slice_in_dim(segment, start, BLOCK, 0)
        pos_rows = start + jnp.arange(BLOCK, dtype=jnp.int32)
        mask = (seg_rows[:, None] == segment[None, :]) & (positions[None, :] <= pos_rows[:, None])
        raw = jnp.einsum("qhd,khd->hqk", q_rows, key_h, preferred_element_type=jnp.float32) * scale
        return jnp.where(mask[None], raw, -1e30)

    def attend(start):
        q_rows = lax.dynamic_slice_in_dim(query_h, start, BLOCK, 0)
        scores = block_scores(q_rows, start)
        peak = jnp.max(scores, axis=-1, keepdims=True)
        expo = jnp.exp(scores - peak)
        total = jnp.sum(expo, axis=-1, keepdims=True)
        probs_b = (expo / total).astype(jnp.bfloat16)
        mixed_rows = jnp.einsum(
            "hqk,khd->qhd", probs_b, value_h, preferred_element_type=jnp.float32
        ).astype(jnp.bfloat16)
        return (mixed_rows, (peak + jnp.log(total))[..., 0])

    starts = jnp.arange(block_count, dtype=jnp.int32) * BLOCK
    mixed_h, log_totals = lax.map(attend, starts)
    mixed_h = mixed_h.reshape(stream_len, 1, local_heads * head_size)
    mixed_b = lax.all_to_all(mixed_h, "seq", split_axis=0, concat_axis=1, tiled=True).reshape(
        rows, width
    )
    h1 = x_in + jnp.dot(mixed_b, wo, preferred_element_type=jnp.float32)
    ffn_set = (
        lax.all_gather(norm2_gain, ("dp", "seq"), axis=0, tiled=True),
        lax.all_gather(w_gate, ("dp", "seq"), axis=0, tiled=True),
        lax.all_gather(w_up, ("dp", "seq"), axis=0, tiled=True),
        lax.all_gather(w_down, ("dp", "seq"), axis=0, tiled=True),
    )
    gain2, wg, wu, wd = ffn_set
    gain2_f = gain2.astype(jnp.float32)
    normed2, inverse2 = norm_forward(h1, gain2_f)
    normed2_b = normed2.astype(jnp.bfloat16)
    gate = jnp.dot(normed2_b, wg, preferred_element_type=jnp.float32)
    up_proj = jnp.dot(normed2_b, wu, preferred_element_type=jnp.float32)
    sigma = jax.nn.sigmoid(gate)
    active = gate * sigma
    hidden_b = (active * up_proj).astype(jnp.bfloat16)
    result = h1 + jnp.dot(hidden_b, wd, preferred_element_type=jnp.float32)
    layer_out = result.astype(jnp.bfloat16).reshape(1, rows, width)
    again_attn = (
        lax.all_gather(norm1_gain, ("dp", "seq"), axis=0, tiled=True),
        lax.all_gather(w_query, ("dp", "seq"), axis=0, tiled=True),
        lax.all_gather(w_key, ("dp", "seq"), axis=0, tiled=True),
        lax.all_gather(w_value, ("dp", "seq"), axis=0, tiled=True),
        lax.all_gather(w_out, ("dp", "seq"), axis=0, tiled=True),
    )
    wq2, wk2, wv2, wo2 = (again_attn[1], again_attn[2], again_attn[3], again_attn[4])
    again_ffn = (
        lax.all_gather(norm2_gain, ("dp", "seq"), axis=0, tiled=True),
        lax.all_gather(w_gate, ("dp", "seq"), axis=0, tiled=True),
        lax.all_gather(w_up, ("dp", "seq"), axis=0, tiled=True),
        lax.all_gather(w_down, ("dp", "seq"), axis=0, tiled=True),
    )
    wg2, wu2, wd2 = (again_ffn[1], again_ffn[2], again_ffn[3])
    grad_y_b = cotangent[0]
    grad_y = grad_y_b.astype(jnp.float32)
    grad_wd = matmul_left(hidden_b, grad_y_b)
    grad_hidden = matmul_right(grad_y_b, wd2)
    grad_gate_b = (grad_hidden * up_proj * sigma * (1.0 + gate * (1.0 - sigma))).astype(
        jnp.bfloat16
    )
    grad_up_b = (grad_hidden * active).astype(jnp.bfloat16)
    grad_wg = matmul_left(normed2_b, grad_gate_b)
    grad_wu = matmul_left(normed2_b, grad_up_b)
    grad_n2 = matmul_right(grad_gate_b, wg2) + matmul_right(grad_up_b, wu2)
    grad_h1_norm, grad_g2 = norm_backward(h1, inverse2, gain2_f, grad_n2)
    grad_h1 = grad_y + grad_h1_norm
    grad_att_b = grad_h1.astype(jnp.bfloat16)
    grad_wo = matmul_left(mixed_b, grad_att_b)
    grad_mixed_b = matmul_right(grad_att_b, wo2).astype(jnp.bfloat16)
    grad_mixed_h = head_layout(
        lax.all_to_all(slice_layout(grad_mixed_b), "seq", split_axis=1, concat_axis=0, tiled=True)
    )

    def attend_back(carry, item):
        acc_key, acc_value = carry
        start, lse_rows = item
        q_rows = lax.dynamic_slice_in_dim(query_h, start, BLOCK, 0)
        d_rows = lax.dynamic_slice_in_dim(grad_mixed_h, start, BLOCK, 0)
        probs = jnp.exp(block_scores(q_rows, start) - lse_rows[..., None])
        grad_probs = jnp.einsum("qhd,khd->hqk", d_rows, value_h, preferred_element_type=jnp.float32)
        inner = jnp.sum(probs * grad_probs, axis=-1, keepdims=True)
        grad_scores = (probs * (grad_probs - inner)).astype(jnp.bfloat16)
        grad_q_rows = (
            jnp.einsum("hqk,khd->qhd", grad_scores, key_h, preferred_element_type=jnp.float32)
            * scale
        ).astype(jnp.bfloat16)
        acc_key = (
            acc_key
            + jnp.einsum("hqk,qhd->khd", grad_scores, q_rows, preferred_element_type=jnp.float32)
            * scale
        )
        acc_value = acc_value + jnp.einsum(
            "hqk,qhd->khd", probs.astype(jnp.bfloat16), d_rows, preferred_element_type=jnp.float32
        )
        return ((acc_key, acc_value), grad_q_rows)

    empty = jnp.zeros((stream_len, local_heads, head_size), jnp.float32)
    (acc_key, acc_value), grad_q_h = lax.scan(attend_back, (empty, empty), (starts, log_totals))
    flat_width = local_heads * head_size
    grad_q_h = grad_q_h.reshape(stream_len, 1, flat_width)
    grad_k_h = acc_key.astype(jnp.bfloat16).reshape(stream_len, 1, flat_width)
    grad_v_h = acc_value.astype(jnp.bfloat16).reshape(stream_len, 1, flat_width)
    grad_q_s, grad_k_s, grad_v_s = (
        lax.all_to_all(grad_q_h, "seq", split_axis=0, concat_axis=1, tiled=True),
        lax.all_to_all(grad_k_h, "seq", split_axis=0, concat_axis=1, tiled=True),
        lax.all_to_all(grad_v_h, "seq", split_axis=0, concat_axis=1, tiled=True),
    )

    def unrotate(t):
        heads_form = t.astype(jnp.float32).reshape(rows, H, head_size)
        return rotate(heads_form, cos_tab, sin_tab, -1.0).astype(jnp.bfloat16).reshape(rows, width)

    grad_qlin_b = unrotate(grad_q_s)
    grad_klin_b = unrotate(grad_k_s)
    half_value = (0.5 * grad_v_s.astype(jnp.float32).reshape(rows, width)).astype(jnp.bfloat16)
    grad_first = half_value.reshape(1, rows, width)
    grad_wq = matmul_left(normed1_b, grad_qlin_b)
    grad_wk = matmul_left(normed1_b, grad_klin_b)
    grad_wv = matmul_left(normed1_b, half_value)
    grad_n1 = (
        matmul_right(grad_qlin_b, wq2)
        + matmul_right(grad_klin_b, wk2)
        + matmul_right(half_value, wv2)
    )
    grad_x_norm, grad_g1 = norm_backward(x_in, inverse1, gain1_f, grad_n1)
    grad_tokens = (grad_h1 + grad_x_norm).astype(jnp.bfloat16).reshape(1, rows, width)
    attn_part = (
        lax.psum_scatter(
            seq_major(grad_g1, outer, groups).astype(jnp.bfloat16),
            "seq",
            scatter_dimension=0,
            tiled=True,
        ).astype(jnp.float32),
        lax.psum_scatter(
            seq_major(grad_wq, outer, groups).astype(jnp.bfloat16),
            "seq",
            scatter_dimension=0,
            tiled=True,
        ).astype(jnp.float32),
        lax.psum_scatter(
            seq_major(grad_wk, outer, groups).astype(jnp.bfloat16),
            "seq",
            scatter_dimension=0,
            tiled=True,
        ).astype(jnp.float32),
        lax.psum_scatter(
            seq_major(grad_wv, outer, groups).astype(jnp.bfloat16),
            "seq",
            scatter_dimension=0,
            tiled=True,
        ).astype(jnp.float32),
        lax.psum_scatter(
            seq_major(grad_wo, outer, groups).astype(jnp.bfloat16),
            "seq",
            scatter_dimension=0,
            tiled=True,
        ).astype(jnp.float32),
    )
    attn_red = (
        lax.psum_scatter(
            attn_part[0].astype(jnp.bfloat16), "dp", scatter_dimension=0, tiled=True
        ).astype(jnp.float32),
        lax.psum_scatter(
            attn_part[1].astype(jnp.bfloat16), "dp", scatter_dimension=0, tiled=True
        ).astype(jnp.float32),
        lax.psum_scatter(
            attn_part[2].astype(jnp.bfloat16), "dp", scatter_dimension=0, tiled=True
        ).astype(jnp.float32),
        lax.psum_scatter(
            attn_part[3].astype(jnp.bfloat16), "dp", scatter_dimension=0, tiled=True
        ).astype(jnp.float32),
        lax.psum_scatter(
            attn_part[4].astype(jnp.bfloat16), "dp", scatter_dimension=0, tiled=True
        ).astype(jnp.float32),
    )
    ffn_part = (
        lax.psum_scatter(
            seq_major(grad_g2, outer, groups).astype(jnp.bfloat16),
            "seq",
            scatter_dimension=0,
            tiled=True,
        ).astype(jnp.float32),
        lax.psum_scatter(
            seq_major(grad_wg, outer, groups).astype(jnp.bfloat16),
            "seq",
            scatter_dimension=0,
            tiled=True,
        ).astype(jnp.float32),
        lax.psum_scatter(
            seq_major(grad_wu, outer, groups).astype(jnp.bfloat16),
            "seq",
            scatter_dimension=0,
            tiled=True,
        ).astype(jnp.float32),
        lax.psum_scatter(
            seq_major(grad_wd, outer, groups).astype(jnp.bfloat16),
            "seq",
            scatter_dimension=0,
            tiled=True,
        ).astype(jnp.float32),
    )
    ffn_red = (
        lax.psum_scatter(
            ffn_part[0].astype(jnp.bfloat16), "dp", scatter_dimension=0, tiled=True
        ).astype(jnp.float32),
        lax.psum_scatter(
            ffn_part[1].astype(jnp.bfloat16), "dp", scatter_dimension=0, tiled=True
        ).astype(jnp.float32),
        lax.psum_scatter(
            ffn_part[2].astype(jnp.bfloat16), "dp", scatter_dimension=0, tiled=True
        ).astype(jnp.float32),
        lax.psum_scatter(
            ffn_part[3].astype(jnp.bfloat16), "dp", scatter_dimension=0, tiled=True
        ).astype(jnp.float32),
    )
    return (
        layer_out,
        grad_tokens,
        grad_first,
        attn_red[0],
        attn_red[1],
        attn_red[2],
        attn_red[3],
        attn_red[4],
        ffn_red[0],
        ffn_red[1],
        ffn_red[2],
        ffn_red[3],
    )


MESH = pl.DeviceIdType.MESH
CHIPS = 8
BF = jnp.bfloat16
F32 = jnp.float32


def place():
    x = lax.axis_index("seq")
    dp = lax.axis_index("dp")
    core = lax.rem(dp, 2)
    chip = lax.div(dp, 2)
    y = lax.rem(chip, 2)
    z = lax.div(chip, 2)
    pos = z * (1 - y) + (CHIPS - 1 - z) * y
    return x, dp, core, chip, pos


def chip_at(pos):
    pos = lax.rem(pos + 2 * CHIPS, CHIPS)
    half = CHIPS // 2
    y = lax.div(pos, half)
    z = pos * (1 - y) + (CHIPS - 1 - pos) * y
    return 2 * z + y


def greet(peers):
    bar = pltpu.get_barrier_semaphore()
    for peer in peers:
        pl.semaphore_signal(bar, inc=1, device_id=peer, device_id_type=MESH)
    pl.semaphore_wait(bar, len(peers))


COLS = (0, 1, 2, 3)
ROWS = (4, 5)


def block_of(buf, t, chip, core, way):
    if t in COLS:
        return buf.at[2 * chip + core, way]
    return buf.at[chip, core, way]


def gather_kernel(*refs):
    ins = refs[0:6]
    bufs = refs[6:12]
    ring_s, ring_r, mate_s, mate_r, swap_s, swap_r, local = refs[12:]
    x, dp, core, chip, pos = place()
    right = (2 * chip_at(pos + 1) + core, x)
    left = (2 * chip_at(pos - 1) + core, x)
    mate = (2 * chip + 1 - core, x)
    across = (dp, 1 - x)
    diagonal = (2 * chip + 1 - core, 1 - x)
    greet((right, left, mate, across, diagonal))

    def swap(t):
        if t == 0:
            src, dst, to = ins[t], bufs[t].at[dp, x], across
        elif t in COLS:
            src, dst, to = ins[t].at[1 - x], bufs[t].at[dp, x], across
        else:
            src, dst, to = ins[t], bufs[t].at[chip, x], diagonal
        return pltpu.make_async_remote_copy(
            src_ref=src, dst_ref=dst, send_sem=swap_s.at[t], recv_sem=swap_r.at[t],
            device_id=to, device_id_type=MESH)

    def keep(t):
        if t == 0:
            src, dst = ins[t], bufs[t].at[dp, x]
        elif t in COLS:
            src, dst = ins[t].at[x], bufs[t].at[dp, x]
        else:
            src, dst = ins[t], bufs[t].at[chip, x]
        return pltpu.make_async_copy(src, dst, local.at[t])

    def hop(t, step, way):
        origin = chip_at(pos - step) if way == 0 else chip_at(pos + step)
        block = block_of(bufs[t], t, origin, core, way)
        return pltpu.make_async_remote_copy(
            src_ref=block, dst_ref=block, send_sem=ring_s.at[t, step, way],
            recv_sem=ring_r.at[t, step, way], device_id=right if way == 0 else left,
            device_id_type=MESH)

    def share(t, step, way):
        origin = chip_at(pos - step) if way == 0 else chip_at(pos + step)
        block = block_of(bufs[t], t, origin, core, way)
        return pltpu.make_async_remote_copy(
            src_ref=block, dst_ref=block, send_sem=mate_s.at[t, step, way],
            recv_sem=mate_r.at[t, step, way], device_id=mate, device_id_type=MESH)

    for t in COLS:
        swap(t).start()
        keep(t).start()
    for t in ROWS:
        @pl.when(core != x)
        def _():
            swap(t).start()

        @pl.when(core == x)
        def _():
            keep(t).start()
    for t in COLS:
        keep(t).wait()
        swap(t).wait()
    for t in ROWS:
        @pl.when(core != x)
        def _():
            swap(t).wait()

        @pl.when(core == x)
        def _():
            keep(t).wait()
    for step in range(CHIPS):
        for t in COLS + ROWS:
            for way in (0, 1):
                if step > 0:
                    hop(t, step - 1, way).wait_recv()
                if step < CHIPS - 1:
                    hop(t, step, way).start()
                share(t, step, way).start()
    for step in range(CHIPS):
        for t in COLS + ROWS:
            for way in (0, 1):
                if step < CHIPS - 1:
                    hop(t, step, way).wait_send()
                share(t, step, way).wait()


def gather_weights(ins):
    gains, qkv, gate, up, out, down = ins
    shapes = [(2 * CHIPS, 2) + gains.shape]
    for w in (qkv, gate, up):
        shapes.append((2 * CHIPS, 2) + w.shape[1:])
    shapes.append((CHIPS, 2) + out.shape)
    shapes.append((CHIPS, 2) + down.shape)
    anywhere = pl.BlockSpec(memory_space=pl.ANY)
    return pl.pallas_call(
        gather_kernel,
        out_shape=[jax.ShapeDtypeStruct(s, BF) for s in shapes],
        in_specs=[anywhere] * 6,
        out_specs=[anywhere] * 6,
        scratch_shapes=[pltpu.SemaphoreType.DMA((6, CHIPS, 2))] * 4
        + [pltpu.SemaphoreType.DMA((6,))] * 3,
        compiler_params=pltpu.CompilerParams(collective_id=0, has_side_effects=True),
    )(*ins)


def scatter_kernel(*refs):
    parts = refs[0:6]
    outs = refs[6:12]
    own = refs[12:18]
    from_mate = refs[18:24]
    landing = refs[24:30]
    swapped = refs[30:36]
    ring_s, ring_r, mate_s, mate_r, swap_s, swap_r, local = refs[36:]
    x, dp, core, chip, pos = place()
    right = (2 * chip_at(pos + 1) + core, x)
    left = (2 * chip_at(pos - 1) + core, x)
    mate = (2 * chip + 1 - core, x)
    across = (dp, 1 - x)
    diagonal = (2 * chip + 1 - core, 1 - x)

    def load(t):
        return pltpu.make_async_copy(parts[t].at[:, core], own[t], local.at[t])

    def share(t):
        return pltpu.make_async_remote_copy(
            src_ref=parts[t].at[:, 1 - core], dst_ref=from_mate[t], send_sem=mate_s.at[t],
            recv_sem=mate_r.at[t], device_id=mate, device_id_type=MESH)

    def hop(t, step, way):
        dest = chip_at(pos - 1 - step) if way == 0 else chip_at(pos + 1 + step)
        return pltpu.make_async_remote_copy(
            src_ref=own[t].at[dest, way], dst_ref=landing[t].at[step, way],
            send_sem=ring_s.at[t, step, way], recv_sem=ring_r.at[t, step, way],
            device_id=right if way == 0 else left, device_id_type=MESH)

    def swap(t):
        if t in COLS:
            return pltpu.make_async_remote_copy(
                src_ref=own[t].at[chip, 1 - x], dst_ref=swapped[t], send_sem=swap_s.at[t],
                recv_sem=swap_r.at[t], device_id=across, device_id_type=MESH)
        return pltpu.make_async_remote_copy(
            src_ref=own[t].at[chip], dst_ref=swapped[t], send_sem=swap_s.at[t],
            recv_sem=swap_r.at[t], device_id=diagonal, device_id_type=MESH)

    order = ROWS + COLS
    for t in order:
        load(t).start()
    greet((right, left, mate, across, diagonal))
    for t in order:
        share(t).start()
    for t in order:
        load(t).wait()
        share(t).wait_recv()
        for step in range(CHIPS):
            for way in (0, 1):
                dest = chip_at(pos - 1 - step) if way == 0 else chip_at(pos + 1 + step)
                mine = own[t][dest, way].astype(F32) + from_mate[t][dest, way].astype(F32)
                own[t][dest, way] = mine.astype(own[t].dtype)
                if step == 0:
                    hop(t, 0, way).start()
    for step in range(1, CHIPS):
        for t in order:
            for way in (0, 1):
                hop(t, step - 1, way).wait_recv()
                dest = chip_at(pos - 1 - step) if way == 0 else chip_at(pos + 1 + step)
                mine = own[t][dest, way].astype(F32) + landing[t][step - 1, way].astype(F32)
                own[t][dest, way] = mine.astype(own[t].dtype)
                if step < CHIPS - 1:
                    hop(t, step, way).start()
    for t in COLS:
        swap(t).start()
    for t in ROWS:
        @pl.when(core != x)
        def _():
            swap(t).start()
    for t in COLS:
        swap(t).wait()
        mine = own[t][chip, x].astype(F32)
        other = swapped[t][...].astype(F32)
        if t == 0:
            outs[t][...] = mine + other
        else:
            outs[t][x] = mine
            outs[t][1 - x] = other
    for t in ROWS:
        @pl.when(core != x)
        def _():
            swap(t).wait()
            outs[t][...] = swapped[t][...].astype(F32)

        @pl.when(core == x)
        def _():
            outs[t][...] = own[t][chip].astype(F32)
    for t in order:
        share(t).wait_send()
        for step in range(CHIPS - 1):
            for way in (0, 1):
                hop(t, step, way).wait_send()


def scatter_grads(parts):
    anywhere = pl.BlockSpec(memory_space=pl.ANY)
    inner = [p.shape[3:] for p in parts]
    kinds = [p.dtype for p in parts]
    outs, swaps = [], []
    for t in range(6):
        if t == 0:
            outs.append(inner[t])
            swaps.append(inner[t])
        elif t in COLS:
            outs.append((2,) + inner[t])
            swaps.append(inner[t])
        else:
            outs.append((2,) + inner[t])
            swaps.append((2,) + inner[t])
    return pl.pallas_call(
        scatter_kernel,
        out_shape=[jax.ShapeDtypeStruct(s, F32) for s in outs],
        in_specs=[anywhere] * 6,
        out_specs=[pl.BlockSpec(memory_space=pltpu.VMEM)] * 6,
        scratch_shapes=[pltpu.VMEM((CHIPS, 2) + s, d) for s, d in zip(inner, kinds)]
        + [pltpu.VMEM((CHIPS, 2) + s, d) for s, d in zip(inner, kinds)]
        + [pltpu.VMEM((CHIPS - 1, 2) + s, d) for s, d in zip(inner, kinds)]
        + [pltpu.VMEM(s, d) for s, d in zip(swaps, kinds)]
        + [pltpu.SemaphoreType.DMA((6, CHIPS, 2))] * 2
        + [pltpu.SemaphoreType.DMA((6,))] * 5,
        compiler_params=pltpu.CompilerParams(
            collective_id=1, has_side_effects=True, vmem_limit_bytes=60 * 2**20),
    )(*parts)


def by_parity(w, groups, unit):
    return w.reshape(w.shape[0], groups, 2, unit).transpose(2, 0, 1, 3).reshape(
        2, w.shape[0], groups * unit)


def from_parity(w, groups, unit):
    return w.reshape(2, w.shape[1], groups, unit).transpose(1, 2, 0, 3).reshape(
        w.shape[1], groups * 2 * unit)


def per_pair(
    tokens, first_values, doc_ids, cotangent, norm1_gain, w_query, w_key, w_value, w_out,
    norm2_gain, w_gate, w_up, w_down,
):
    x = lax.axis_index("seq")
    dp = lax.axis_index("dp")
    rows, width = tokens.shape[1:]
    stream = 2 * rows
    head = width // H
    heads = H // 2
    flat = heads * head
    units = w_gate.shape[1] // 2
    unit = units // CHIPS
    share = norm1_gain.shape[0]

    def flip(t):
        return lax.ppermute(t, "seq", [(0, 1), (1, 0)])

    def both(t):
        other = flip(t)
        pair = jnp.stack([t, other])
        return jnp.where(x == 0, pair, pair[::-1]).reshape((2 * t.shape[0],) + t.shape[1:])

    def mine(t):
        return lax.dynamic_slice_in_dim(t, x * rows, rows, 0)

    def theirs(t):
        return lax.dynamic_slice_in_dim(t, (1 - x) * rows, rows, 0)

    def summed(t):
        return mine(t) + flip(theirs(t).astype(BF)).astype(F32)

    lanes = 128
    per_tile = lanes // share
    seat = lax.rem(2 * dp + x, per_tile)
    lane = lax.broadcasted_iota(jnp.int32, (1, lanes), 1)

    def seated(g):
        return jnp.where(lane // share == seat, jnp.tile(g, per_tile)[None], 0).astype(BF)

    tile = jnp.concatenate([seated(norm1_gain), seated(norm2_gain), jnp.zeros((6, lanes), BF)])
    qkv_in = jnp.concatenate([by_parity(w, heads, head) for w in (w_query, w_key, w_value)], axis=2)
    half = w_out.shape[0] // 2
    out_in = w_out.reshape(2, half, width)
    down_in = w_down.reshape(w_down.shape[0], 2, width // 2).transpose(1, 0, 2)
    gains, wqkv, wg, wu, wo, wd = gather_weights(
        (tile, qkv_in, by_parity(w_gate, CHIPS, unit), by_parity(w_up, CHIPS, unit), out_in, down_in))
    gains = gains.reshape(width // lanes, per_tile, 8, lanes).astype(F32).sum(1)
    gain1 = gains[:, 0].reshape(width)
    gain2 = gains[:, 1].reshape(width)
    wqkv = wqkv.reshape(width, 3 * flat)
    wg = wg.reshape(width, units)
    wu = wu.reshape(width, units)
    wo = wo.reshape(flat, width)
    wd = wd.transpose(0, 1, 3, 2, 4).reshape(units, width)

    tok = both(tokens[0])
    x_all = tok.astype(F32)
    normed1, inverse1 = norm_forward(x_all, gain1)
    n1 = normed1.astype(BF)
    qkv = jnp.dot(n1, wqkv, preferred_element_type=F32).reshape(stream, 3, heads, head)
    cos_tab, sin_tab = rope_tables(0, stream, head)
    query = rotate(qkv[:, 0], cos_tab, sin_tab, 1.0).astype(BF)
    key = rotate(qkv[:, 1], cos_tab, sin_tab, 1.0).astype(BF)
    first2 = by_parity(first_values[0], heads, head)
    first_mine = lax.dynamic_index_in_dim(first2, x, 0, keepdims=False)
    first_theirs = flip(lax.dynamic_index_in_dim(first2, 1 - x, 0, keepdims=False))
    pair = jnp.stack([first_mine, first_theirs])
    first = jnp.where(x == 0, pair, pair[::-1]).reshape(stream, heads, head)
    value = (0.5 * (qkv[:, 2] + first.astype(F32))).astype(BF)
    segment = doc_ids[0]
    positions = jnp.arange(stream, dtype=jnp.int32)
    mask = (segment[:, None] == segment[None, :]) & (positions[None, :] <= positions[:, None])
    scale = head ** (-0.5)
    scores = jnp.einsum("qhd,khd->hqk", query, key, preferred_element_type=F32) * scale
    scores = jnp.where(mask[None], scores, -1e30)
    peak = jnp.max(scores, axis=-1, keepdims=True)
    expo = jnp.exp(scores - peak)
    probs = expo / jnp.sum(expo, axis=-1, keepdims=True)
    probs_b = probs.astype(BF)
    mixed = jnp.einsum("hqk,khd->qhd", probs_b, value, preferred_element_type=F32).astype(BF)
    mixed = mixed.reshape(stream, flat)
    h1 = mine(x_all) + summed(jnp.dot(mixed, wo, preferred_element_type=F32))
    normed2, inverse2 = norm_forward(h1, gain2)
    n2 = both(normed2.astype(BF))
    gate = jnp.dot(n2, wg, preferred_element_type=F32)
    up = jnp.dot(n2, wu, preferred_element_type=F32)
    sigma = jax.nn.sigmoid(gate)
    active = gate * sigma
    hidden = (active * up).astype(BF)
    layer_out = (h1 + summed(jnp.dot(hidden, wd, preferred_element_type=F32))).astype(BF)[None]
    dy = both(cotangent[0])
    grad_wd = matmul_left(hidden, dy).astype(BF)
    g_hidden = matmul_right(dy, wd)
    g_gate = (g_hidden * up * sigma * (1.0 + gate * (1.0 - sigma))).astype(BF)
    g_up = (g_hidden * active).astype(BF)
    grad_wg = matmul_left(n2, g_gate).astype(BF)
    grad_wu = matmul_left(n2, g_up).astype(BF)
    g_n2 = summed(matmul_right(g_gate, wg) + matmul_right(g_up, wu))
    g_h1_norm, grad_g2 = norm_backward(h1, inverse2, gain2, g_n2)
    g_h1 = mine(dy).astype(F32) + g_h1_norm
    g_att = both(g_h1.astype(BF))
    grad_wo = matmul_left(mixed, g_att).astype(BF)
    g_mixed = matmul_right(g_att, wo).astype(BF).reshape(stream, heads, head)
    g_probs = jnp.einsum("qhd,khd->hqk", g_mixed, value, preferred_element_type=F32)
    delta = jnp.sum(probs * g_probs, axis=-1, keepdims=True)
    g_scores = (probs * (g_probs - delta)).astype(BF)
    g_query = (jnp.einsum("hqk,khd->qhd", g_scores, key, preferred_element_type=F32) * scale)
    g_key = (jnp.einsum("hqk,qhd->khd", g_scores, query, preferred_element_type=F32) * scale)
    g_value = jnp.einsum("hqk,qhd->khd", probs_b, g_mixed, preferred_element_type=F32)

    def unrotate(t):
        t = t.astype(BF).astype(F32)
        return rotate(t, cos_tab, sin_tab, -1.0).astype(BF).reshape(stream, flat)

    g_vlin = (0.5 * g_value).astype(BF).reshape(stream, flat)
    g_lin = jnp.concatenate([unrotate(g_query), unrotate(g_key), g_vlin], axis=1)
    grad_wqkv = matmul_left(n1, g_lin).astype(BF)
    g_n1 = summed(matmul_right(g_lin, wqkv))
    g_x, grad_g1 = norm_backward(mine(x_all), mine(inverse1), gain1, g_n1)
    grad_tokens = (g_h1 + g_x).astype(BF)[None]
    gv_mine = mine(g_vlin)
    gv_theirs = flip(theirs(g_vlin))
    pair = jnp.stack([gv_mine, gv_theirs])
    grad_first = from_parity(jnp.where(x == 0, pair, pair[::-1]), heads, head)[None]

    chunks = jnp.stack([grad_g1, grad_g2]).reshape(2, width // lanes, lanes).transpose(1, 0, 2)
    chunks = jnp.pad(chunks, ((0, 0), (0, 6), (0, 0)))
    gain_parts = jnp.repeat(chunks, per_tile, axis=0)
    devs = 2 * CHIPS
    out = scatter_grads((
        gain_parts.reshape(CHIPS, 2, 2, 8, lanes),
        grad_wqkv.reshape(CHIPS, 2, 2, share, 3 * flat),
        grad_wg.reshape(CHIPS, 2, 2, share, units),
        grad_wu.reshape(CHIPS, 2, 2, share, units),
        grad_wo.reshape(CHIPS, 2, 2, half, width),
        grad_wd.reshape(CHIPS, 2, w_down.shape[0], 2, width // 2).transpose(0, 1, 3, 2, 4),
    ))
    g12 = lax.dynamic_slice_in_dim(out[0], seat * share, share, 1)
    gq, gk, gv = [from_parity(out[1][:, :, i * flat:(i + 1) * flat], heads, head) for i in range(3)]
    return (
        layer_out, grad_tokens, grad_first, g12[0], gq, gk, gv, out[4].reshape(2 * half, width),
        g12[1], from_parity(out[2], CHIPS, unit), from_parity(out[3], CHIPS, unit),
        out[5].transpose(1, 0, 2).reshape(w_down.shape[0], width),
    )


def solution(mesh):
    on_ring = mesh.shape["dp"] == 2 * CHIPS and mesh.shape["seq"] == 2
    placed = (
        P("dp", "seq", None),
        P("dp", "seq", None),
        P("dp", None),
        P("dp", "seq", None),
        P(("dp", "seq")),
        P(("dp", "seq"), None),
        P(("dp", "seq"), None),
        P(("dp", "seq"), None),
        P(("dp", "seq"), None),
        P(("dp", "seq")),
        P(("dp", "seq"), None),
        P(("dp", "seq"), None),
        P(("dp", "seq"), None),
    )
    return jax.shard_map(
        per_pair if on_ring else per_device,
        mesh=mesh,
        in_specs=placed,
        out_specs=placed[:2] + placed[3:],
        check_vma=False,
    )
```
